32 devices in a mesh: section: 2 (over x), req: 8 (over z, y), head: 2 (over core).
Axes of the slice: x: 2, y: 2, z: 4, core: 2. Of those that a mesh axis runs over, the one named last changes fastest.
Arguments:
- latent_tokens: bfloat16 [8, 2, 256, 1536], P('req', None, 'head'), may hold values from -6 to 6
- w_qkv: bfloat16 [2, 1536, 4608], P('section', 'req', 'head'), may hold values from -0.15625 to 0.15625
- w_out: bfloat16 [2, 1536, 1536], P('section', 'head', 'req'), may hold values from -0.75 to 0.75
- time_mod: float32 [2, 28, 3, 1536], P('section'), may hold values from -3 to 3
- text_mod: float32 [2, 8, 2, 3, 1536], P('section', 'req'), may hold values from -3 to 3
- stale_kv: bfloat16 [2, 8, 2, 1178, 3072], P('section', 'req', None, None, 'head'), may hold values from -150 to 150
- guided: int32 [8], P('req'), may hold values 0 or 1
- patch_index: int32 [8], P('req'), may hold values from 0 to 3
- timestep: int32 [8], P('req'), may hold values from 0 to 27
Outputs:
- hidden_out: bfloat16 [2, 8, 2, 256, 1536], P('section', 'req', None, 'head')
- fresh_kv: bfloat16 [2, 8, 2, 256, 3072], P('section', 'req', None, None, 'head')
The draws below stay inside these ranges and needn't reach their ends.
All inputs are finite; a program needn't handle non-finite values. No bound on the sum of `guided` on one device may be relied on, other than what follows from the above.
Results may differ from the reference program's by a relative error of at most 0.04.
Values may be sent and summed in bfloat16 or wider, within the bound.
A program may use at most 192 MiB of HBM per device.

```python
import jax
import jax.numpy as jnp
from jax import lax

D = 1536
HEADS = 24
HD = 64
PATCH = 256
PATCHES = 4
TSTEPS = 28
LAYERS = 2
REQS = 8
STALE = 1178
N_HEAD = 2


def draw_stale_kv(key, part):
    shape = (LAYERS, REQS, 2, STALE, 2 * D)
    base = jnp.clip(jax.random.normal(key, shape, jnp.float32), -6.0, 6.0)
    return base.astype(jnp.bfloat16)


def with_ends(entries, stream_key, low, top_value):
    place = [jax.random.randint(jax.random.fold_in(stream_key, axis), (), 0, length) for axis, length in enumerate(entries.shape)]
    main_axis = entries.shape.index(max(entries.shape))
    next_to = place[:main_axis] + [(place[main_axis] + 1) % entries.shape[main_axis]] + place[main_axis + 1:]
    return entries.at[tuple(place)].set(low).at[tuple(next_to)].set(top_value)


def block_scale(rng, shape, pieces, smallest, high):
    factor_of, own = 1.0, jax.random.fold_in(rng, 6)
    for dim, blocks in pieces:
        steps = jnp.exp(jax.random.uniform(jax.random.fold_in(own, dim), (blocks,), jnp.float32, smallest / len(pieces), high / len(pieces)))
        factor_of = factor_of * jnp.repeat(steps, shape[dim] // blocks).reshape([-1 if axis == dim else 1 for axis in range(len(shape))])
    return factor_of


def scatter_about(key, dims, deviation, bound, shards=(), kind=jnp.bfloat16):
    gain = block_scale(key, dims, shards, -0.22, 0.18) if shards else 1.0
    array = jax.random.normal(key, dims, jnp.float32) * deviation * gain
    return jnp.minimum(jnp.maximum(array, -bound), bound).astype(kind)


def setup_inputs(seed: int = 0) -> dict:
    seeds = jax.random.split(jax.random.key(seed), 10)
    latent_tokens = scatter_about(seeds[0], (REQS, 2, PATCH, D), 1.0, 6.0, ((0, 8), (2, 2)))
    w_qkv = scatter_about(seeds[1], (LAYERS, D, 3 * D), D ** -0.5, 0.15625, ((0, 2), (1, 8), (2, 2)))
    w_out = scatter_about(seeds[2], (LAYERS, D, D), HD ** -0.5, 0.75, ((0, 2), (1, 2), (2, 8)))
    time_mod = scatter_about(seeds[3], (LAYERS, TSTEPS, 3, D), 0.5, 3.0, ((0, 2),), jnp.float32)
    text_mod = scatter_about(seeds[4], (LAYERS, REQS, 2, 3, D), 0.5, 3.0, ((0, 2), (1, 8)), jnp.float32)
    stale_kv = draw_stale_kv(jax.random.fold_in(seeds[9], 71), 0)
    guided = with_ends((jax.random.randint(seeds[6], (REQS,), 0, 2) < 1).astype(jnp.int32), jax.random.fold_in(seeds[6], 1), 0, 1)
    patch_index = with_ends(jax.random.randint(seeds[7], (REQS,), 0, PATCHES), jax.random.fold_in(seeds[7], 1), 0, PATCHES - 1).astype(jnp.int32)
    timestep = with_ends(jax.random.randint(seeds[8], (REQS,), 0, TSTEPS), jax.random.fold_in(seeds[8], 1), 0, TSTEPS - 1).astype(jnp.int32)
    return {"latent_tokens": latent_tokens, "w_qkv": w_qkv, "w_out": w_out, "time_mod": time_mod, "text_mod": text_mod, "stale_kv": stale_kv, "guided": guided, "patch_index": patch_index, "timestep": timestep}


def attend(queries, own_keys, own_values, stale_pair, patch_here):
    heads_here = queries.shape[1]
    stale_split = stale_pair.reshape(STALE, heads_here, 2, HD)
    stale_keys = stale_split[:, :, 0]
    stale_values = stale_split[:, :, 1]
    all_keys = jnp.concatenate([own_keys, stale_keys], 0)
    all_values = jnp.concatenate([own_values, stale_values], 0)
    scores = jnp.einsum('qhd,khd->hqk', queries.astype(jnp.float32), all_keys.astype(jnp.float32)) * HD ** (-0.5)
    position = jnp.arange(PATCH + STALE, dtype=jnp.int32)
    stale_pos = position - PATCH
    hidden_key = (stale_pos >= 0) & (stale_pos < PATCHES * PATCH) & (stale_pos // PATCH == patch_here)
    scores = jnp.where(hidden_key[None, None, :], -jnp.inf, scores)
    row_max = lax.optimization_barrier(jnp.max(scores, axis=-1, keepdims=True))
    exponent = jnp.exp(scores - row_max)
    weights = (exponent / lax.optimization_barrier(jnp.sum(exponent, axis=-1, keepdims=True))).astype(jnp.bfloat16)
    mixed_heads = jnp.einsum('hqk,khd->qhd', weights.astype(jnp.float32), all_values.astype(jnp.float32))
    return mixed_heads.astype(jnp.bfloat16).reshape(PATCH, heads_here * HD)

def apply_layer(hidden, qkv_weight, out_weight, modulation, stale_pair, patch_here):
    values_f = hidden.astype(jnp.float32)
    row_mean = lax.optimization_barrier(jnp.mean(values_f, axis=-1, keepdims=True))
    centered = values_f - row_mean
    row_var = lax.optimization_barrier(jnp.mean(centered * centered, axis=-1, keepdims=True))
    normed = (centered * lax.rsqrt(row_var + 1e-06) * (1.0 + modulation[1]) + modulation[0]).astype(jnp.bfloat16)
    projected = jnp.dot(normed, qkv_weight, preferred_element_type=jnp.float32).reshape(PATCH, HEADS, 3, HD)
    queries = projected[:, :, 0].astype(jnp.bfloat16)
    own_keys = projected[:, :, 1].astype(jnp.bfloat16)
    own_values = projected[:, :, 2].astype(jnp.bfloat16)
    mixed_heads = attend(queries, own_keys, own_values, stale_pair, patch_here)
    group_cols = D // N_HEAD
    partials = jnp.einsum('pgf,gfd->gpd', mixed_heads.reshape(PATCH, N_HEAD, group_cols).astype(jnp.float32), out_weight.reshape(N_HEAD, group_cols, D).astype(jnp.float32)).astype(jnp.bfloat16)
    attn_sum = lax.optimization_barrier(jnp.sum(partials.astype(jnp.float32), axis=0))
    updated = (values_f + modulation[2] * attn_sum).astype(jnp.bfloat16)
    fresh_pair = jnp.stack([own_keys, own_values], axis=2).reshape(PATCH, 2 * D)
    return (updated, fresh_pair)

def reference(latent_tokens, w_qkv, w_out, time_mod, text_mod, stale_kv, guided, patch_index, timestep):
    item_count = REQS * 2
    tokens = latent_tokens.reshape(item_count, PATCH, D)
    item_ids = jnp.arange(item_count, dtype=jnp.int32)
    request_of = item_ids // 2
    parity = item_ids % 2
    keep_row = jnp.where((parity == 1) & (guided[request_of] == 0), 0.0, 1.0).astype(jnp.float32)
    modulation = (time_mod[:, timestep][:, :, None] + text_mod).reshape(LAYERS, item_count, 3, D)
    stale_all = stale_kv.reshape(LAYERS, item_count, STALE, 2 * D)
    patch_all = patch_index[request_of]

    def one_item(item_index):
        hidden = tokens[item_index]
        layer_hidden = []
        layer_fresh = []
        for layer_index in range(LAYERS):
            hidden, fresh_pair = apply_layer(hidden, w_qkv[layer_index], w_out[layer_index], modulation[layer_index, item_index], stale_all[layer_index, item_index], patch_all[item_index])
            layer_hidden.append(hidden)
            layer_fresh.append(fresh_pair)
        factor = keep_row[item_index]
        kept_hidden = (jnp.stack(layer_hidden).astype(jnp.float32) * factor).astype(jnp.bfloat16)
        kept_fresh = (jnp.stack(layer_fresh).astype(jnp.float32) * factor).astype(jnp.bfloat16)
        return (kept_hidden, kept_fresh)
    all_hidden, all_fresh = lax.map(one_item, item_ids)
    hidden_out = jnp.transpose(all_hidden, (1, 0, 2, 3)).reshape(LAYERS, REQS, 2, PATCH, D)
    fresh_kv = jnp.transpose(all_fresh, (1, 0, 2, 3)).reshape(LAYERS, REQS, 2, PATCH, 2 * D)
    return (hidden_out, fresh_kv)
```

```python
import functools

import jax
import jax.numpy as jnp
from jax import lax
from jax.experimental import pallas as pl
from jax.experimental.pallas import tpu as pltpu
from jax.sharding import PartitionSpec as P

HD = 64
PATCH = 256
PATCHES = 4
STALE = 1178
TEXT = STALE - PATCHES * PATCH
MESH = pl.DeviceIdType.MESH


def ring_index(place, n):
    return jnp.where(place < n // 2, 2 * place, 2 * (n - 1 - place) + 1)


def gather_kernel(n, qkv_ref, out_ref, qkv_all, out_all, send_sem, recv_sem, own_sem):
    me = lax.axis_index("req")
    place = jnp.where(me % 2 == 0, me // 2, n - 1 - me // 2)
    right = ring_index((place + 1) % n, n)
    left = ring_index((place + n - 1) % n, n)
    barrier = pltpu.get_barrier_semaphore()
    for neighbour in (left, right):
        pl.semaphore_signal(barrier, inc=1, device_id={"req": neighbour}, device_id_type=MESH)
    pl.semaphore_wait(barrier, 2)

    rows = qkv_ref.shape[0]
    out_rows = out_ref.shape[0]
    q_half, o_half = rows // 2, out_rows // 2
    q_cut = (q_half // 2 + 7) // 8 * 8
    pieces = []
    for way in range(2):
        pieces.append(
            (
                (qkv_ref, qkv_all, way * q_half, q_cut),
                (qkv_ref, qkv_all, way * q_half + q_cut, q_half - q_cut),
                (out_ref, out_all, way * o_half, o_half),
            )
        )
    own = (
        pltpu.make_async_copy(qkv_ref, qkv_all.at[me], own_sem.at[0]),
        pltpu.make_async_copy(out_ref, out_all.at[me], own_sem.at[1]),
    )

    def hop(step, way, number):
        source, target, first, count = pieces[way][number]
        owner = ring_index((place + (n - step if way == 0 else step)) % n, n)
        span = pl.ds(first, count)
        block = source.at[span] if step == 0 else target.at[owner, span]
        return pltpu.make_async_remote_copy(
            src_ref=block,
            dst_ref=target.at[owner, span],
            send_sem=send_sem.at[way, number],
            recv_sem=recv_sem.at[step, way, number],
            device_id={"req": right if way == 0 else left},
            device_id_type=MESH,
        )

    for step in range(n - 1):
        for number in range(3):
            for way in range(2):
                if step > 0:
                    before = hop(step - 1, way, number)
                    before.wait_recv()
                    before.wait_send()
                hop(step, way, number).start()
        if step == 0:
            for copy in own:
                copy.start()
    for number in range(3):
        for way in range(2):
            last = hop(n - 2, way, number)
            last.wait_recv()
            last.wait_send()
    for copy in own:
        copy.wait()


def gather_weights(qkv_shard, out_shard):
    n = lax.axis_size("req")
    return pl.pallas_call(
        functools.partial(gather_kernel, n),
        out_shape=(
            jax.ShapeDtypeStruct((n, *qkv_shard.shape), qkv_shard.dtype),
            jax.ShapeDtypeStruct((n, *out_shard.shape), out_shard.dtype),
        ),
        in_specs=[pl.BlockSpec(memory_space=pl.ANY)] * 2,
        out_specs=[pl.BlockSpec(memory_space=pl.ANY)] * 2,
        scratch_shapes=[
            pltpu.SemaphoreType.DMA((2, 3)),
            pltpu.SemaphoreType.DMA((n - 1, 2, 3)),
            pltpu.SemaphoreType.DMA((2,)),
        ],
        compiler_params=pltpu.CompilerParams(collective_id=0, has_side_effects=True),
    )(qkv_shard, out_shard)


def nt_dot(a, b):
    return lax.dot_general(a, b, (((1,), (1,)), ((), ())), preferred_element_type=jnp.float32)


def layer_kernel(
    block_heads, facts, hidden, mod, w_qkv, stale, w_out, *rest
):
    fresh_out, out_terms, normed, total = rest[-4:]
    step = pl.program_id(0)

    @pl.when(step == 0)
    def _():
        values_f = hidden[...].astype(jnp.float32)
        row_mean = jnp.mean(values_f, axis=-1, keepdims=True)
        centered = values_f - row_mean
        row_var = jnp.mean(centered * centered, axis=-1, keepdims=True)
        scaled = centered * lax.rsqrt(row_var + 1e-06)
        normed[...] = (scaled * (1.0 + mod[1:2, :]) + mod[0:1, :]).astype(jnp.bfloat16)

    projected = jnp.dot(normed[...], w_qkv[...], preferred_element_type=jnp.float32).astype(
        jnp.bfloat16
    )
    patch_here = facts[1]
    keep = facts[2].astype(jnp.float32)
    blank = jnp.zeros((PATCH, HD), jnp.bfloat16)
    mixed = []
    for head in range(block_heads):
        query = projected[:, head * 3 * HD : head * 3 * HD + HD]
        pair = projected[:, head * 3 * HD + HD : (head + 1) * 3 * HD]
        lanes = slice(head * 2 * HD, (head + 1) * 2 * HD)
        fresh_out[:, lanes] = (pair.astype(jnp.float32) * keep).astype(jnp.bfloat16)
        query = jnp.concatenate([query * jnp.bfloat16(HD**-0.5), blank], axis=1)
        pairs = [pair]
        for number in range(PATCHES - 1):
            place = number + (number >= patch_here).astype(jnp.int32)
            pairs.append(stale[pl.ds(pl.multiple_of(place * PATCH, PATCH), PATCH), lanes])
        pairs.append(stale[PATCHES * PATCH :, lanes])
        scores = [nt_dot(query, part) for part in pairs]
        top = functools.reduce(
            jnp.maximum, [jnp.max(part, axis=-1, keepdims=True) for part in scores]
        )
        exponent = [jnp.exp(part - top) for part in scores]
        norm = sum(jnp.sum(part, axis=-1, keepdims=True) for part in exponent)
        values = sum(
            jnp.dot(part.astype(jnp.bfloat16), kv, preferred_element_type=jnp.float32)
            for part, kv in zip(exponent, pairs)
        )
        mixed.append((values[:, HD:] / norm).astype(jnp.bfloat16))
    terms = nt_dot(jnp.concatenate(mixed, axis=1), w_out[...])

    @pl.when(step == 0)
    def _():
        total[...] = terms

    @pl.when(step > 0)
    def _():
        total[...] += terms

    @pl.when(step == pl.num_programs(0) - 1)
    def _():
        out_terms[...] = total[...].astype(jnp.bfloat16)


def run_layer(facts, hidden, modulation, w_qkv, stale_kv, w_out, fresh_buf):
    width = hidden.shape[1]
    heads_here = stale_kv.shape[-1] // (2 * HD)
    block_heads = 4 if heads_here % 4 == 0 else heads_here
    items = modulation.shape[0]
    operands = [facts, hidden, modulation, w_qkv, stale_kv, w_out]
    in_specs = [
        pl.BlockSpec((PATCH, width), lambda i, f: (0, 0)),
        pl.BlockSpec((None, 3, width), lambda i, f: (f[0], 0, 0)),
        pl.BlockSpec((width, block_heads * 3 * HD), lambda i, f: (0, i)),
        pl.BlockSpec(
            (None, None, None, STALE, block_heads * 2 * HD),
            lambda i, f: (0, f[0] // 2, f[0] % 2, 0, i),
        ),
        pl.BlockSpec((width, block_heads * HD), lambda i, f: (0, i)),
    ]
    aliases = {}
    if fresh_buf is not None:
        aliases = {len(operands): 0}
        operands.append(fresh_buf)
        in_specs.append(pl.BlockSpec(memory_space=pl.ANY))
    return pl.pallas_call(
        functools.partial(layer_kernel, block_heads),
        out_shape=(
            jax.ShapeDtypeStruct((items, PATCH, heads_here * 2 * HD), jnp.bfloat16),
            jax.ShapeDtypeStruct((PATCH, width), jnp.bfloat16),
        ),
        grid_spec=pltpu.PrefetchScalarGridSpec(
            num_scalar_prefetch=1,
            grid=(heads_here // block_heads,),
            in_specs=in_specs,
            out_specs=[
                pl.BlockSpec((None, PATCH, block_heads * 2 * HD), lambda i, f: (f[0], 0, i)),
                pl.BlockSpec((PATCH, width), lambda i, f: (0, 0)),
            ],
            scratch_shapes=[
                pltpu.VMEM((PATCH, width), jnp.bfloat16),
                pltpu.VMEM((PATCH, width), jnp.float32),
            ],
        ),
        input_output_aliases=aliases,
        compiler_params=pltpu.CompilerParams(vmem_limit_bytes=48 << 20),
    )(*operands)


def shards(
    latent_tokens, w_qkv, w_out, time_mod, text_mod, stale_kv, guided, patch_index, timestep
):
    section_index = lax.axis_index("section")
    sections = lax.axis_size("section")
    requests = latent_tokens.shape[0]
    item_count = 2 * requests
    local_rows, model_width = latent_tokens.shape[2:]
    tokens = latent_tokens.reshape(item_count, local_rows, model_width)
    tokens_full = lax.all_gather(tokens, "head", axis=1, tiled=True)
    per_time = jnp.stack(
        [
            lax.dynamic_index_in_dim(time_mod[0], timestep[i], 0, keepdims=False)
            for i in range(requests)
        ]
    )
    modulation = (per_time[:, None] + text_mod[0]).reshape(item_count, 3, model_width)
    patch_all = jnp.repeat(patch_index, 2)
    guided_all = jnp.repeat(guided, 2)
    parity = jnp.arange(item_count, dtype=jnp.int32) % 2
    keep_all = jnp.where((parity == 1) & (guided_all == 0), 0, 1).astype(jnp.int32)
    qkv_all, out_all = gather_weights(w_qkv[0], w_out[0].T)
    qkv_full = qkv_all.reshape(-1, qkv_all.shape[-1])
    out_full = out_all.reshape(-1, out_all.shape[-1])

    fresh_buf = None
    received = None
    kept = []
    for tick in range(item_count + sections - 1):
        slot = jnp.clip(tick - section_index, 0, item_count - 1)
        layer_in = lax.dynamic_index_in_dim(tokens, slot, 0, keepdims=False)
        hidden = lax.dynamic_index_in_dim(tokens_full, slot, 0, keepdims=False)
        if tick > 0:
            arrived = lax.all_gather(received, "head", axis=0, tiled=True)
            layer_in = jnp.where(section_index == 0, layer_in, received)
            hidden = jnp.where(section_index == 0, hidden, arrived)
        facts = jnp.stack([slot, patch_all[slot], keep_all[slot]]).astype(jnp.int32)
        fresh_buf, out_terms = run_layer(
            facts, hidden, modulation, qkv_full, stale_kv, out_full, fresh_buf
        )
        attn = lax.psum_scatter(out_terms, "head", scatter_dimension=0, tiled=True)
        gate = lax.dynamic_index_in_dim(modulation[:, 2], slot, 0, keepdims=True)
        updated = (
            layer_in.astype(jnp.float32) + gate * attn.astype(jnp.float32)
        ).astype(jnp.bfloat16)
        kept.append(jnp.where(keep_all[slot] == 1, updated, jnp.zeros_like(updated)))
        if tick < item_count + sections - 2:
            received = lax.ppermute(
                updated, "section", [(i, i + 1) for i in range(sections - 1)]
            )
    hidden_out = jnp.stack(
        [jnp.where(section_index == 0, kept[i], kept[i + 1]) for i in range(item_count)]
    ).reshape(1, requests, 2, local_rows, model_width)
    fresh_kv = fresh_buf.reshape(1, requests, 2, PATCH, fresh_buf.shape[-1])
    return (hidden_out, fresh_kv)


def solution(mesh):
    in_specs = (
        P("req", None, "head", None),
        P("section", "req", "head"),
        P("section", "head", "req"),
        P("section", None, None, None),
        P("section", "req", None, None, None),
        P("section", "req", None, None, "head"),
        P("req"),
        P("req"),
        P("req"),
    )
    out_specs = (P("section", "req", None, "head", None), P("section", "req", None, None, "head"))
    return jax.shard_map(shards, mesh=mesh, in_specs=in_specs, out_specs=out_specs, check_vma=False)
```

```python
import functools

import jax
import jax.numpy as jnp
from jax import lax
from jax.experimental import pallas as pl
from jax.experimental.pallas import tpu as pltpu
from jax.sharding import PartitionSpec as P

HD = 64
PATCH = 256
PATCHES = 4
STALE = 1178
TEXT = STALE - PATCHES * PATCH
MESH = pl.DeviceIdType.MESH


def ring_index(place, n):
    return jnp.where(place < n // 2, 2 * place, 2 * (n - 1 - place) + 1)


def gather_kernel(n, qkv_ref, out_ref, qkv_all, out_all, send_sem, recv_sem, own_sem):
    me = lax.axis_index("req")
    place = jnp.where(me % 2 == 0, me // 2, n - 1 - me // 2)
    right = ring_index((place + 1) % n, n)
    left = ring_index((place + n - 1) % n, n)
    barrier = pltpu.get_barrier_semaphore()
    for neighbour in (left, right):
        pl.semaphore_signal(barrier, inc=1, device_id={"req": neighbour}, device_id_type=MESH)
    pl.semaphore_wait(barrier, 2)

    rows = qkv_ref.shape[0]
    out_rows = out_ref.shape[0]
    q_half, o_half = rows // 2, out_rows // 2
    q_cut = (q_half // 2 + 7) // 8 * 8
    pieces = []
    for way in range(2):
        pieces.append(
            (
                (qkv_ref, qkv_all, way * q_half, q_cut),
                (qkv_ref, qkv_all, way * q_half + q_cut, q_half - q_cut),
                (out_ref, out_all, way * o_half, o_half),
            )
        )
    own = (
        pltpu.make_async_copy(qkv_ref, qkv_all.at[me], own_sem.at[0]),
        pltpu.make_async_copy(out_ref, out_all.at[me], own_sem.at[1]),
    )

    def hop(step, way, number):
        source, target, first, count = pieces[way][number]
        owner = ring_index((place + (n - step if way == 0 else step)) % n, n)
        span = pl.ds(first, count)
        block = source.at[span] if step == 0 else target.at[owner, span]
        return pltpu.make_async_remote_copy(
            src_ref=block,
            dst_ref=target.at[owner, span],
            send_sem=send_sem.at[way, number],
            recv_sem=recv_sem.at[step, way, number],
            device_id={"req": right if way == 0 else left},
            device_id_type=MESH,
        )

    for step in range(n - 1):
        for number in range(3):
            for way in range(2):
                if step > 0:
                    before = hop(step - 1, way, number)
                    before.wait_recv()
                    before.wait_send()
                hop(step, way, number).start()
        if step == 0:
            for copy in own:
                copy.start()
    for number in range(3):
        for way in range(2):
            last = hop(n - 2, way, number)
            last.wait_recv()
            last.wait_send()
    for copy in own:
        copy.wait()


def gather_weights(qkv_shard, out_shard):
    n = lax.axis_size("req")
    return pl.pallas_call(
        functools.partial(gather_kernel, n),
        out_shape=(
            jax.ShapeDtypeStruct((n, *qkv_shard.shape), qkv_shard.dtype),
            jax.ShapeDtypeStruct((n, *out_shard.shape), out_shard.dtype),
        ),
        in_specs=[pl.BlockSpec(memory_space=pl.ANY)] * 2,
        out_specs=[pl.BlockSpec(memory_space=pl.ANY)] * 2,
        scratch_shapes=[
            pltpu.SemaphoreType.DMA((2, 3)),
            pltpu.SemaphoreType.DMA((n - 1, 2, 3)),
            pltpu.SemaphoreType.DMA((2,)),
        ],
        compiler_params=pltpu.CompilerParams(collective_id=0, has_side_effects=True),
    )(qkv_shard, out_shard)


def nt_dot(a, b):
    return lax.dot_general(a, b, (((1,), (1,)), ((), ())), preferred_element_type=jnp.float32)


def layer_kernel(
    block_heads, base, facts, hidden, mod, w_qkv, stale, w_out, *rest
):
    fresh_out, out_terms, normed, total = rest[-4:]
    step = pl.program_id(0)

    @pl.when(step == 0)
    def _():
        values_f = hidden[...].astype(jnp.float32)
        row_mean = jnp.mean(values_f, axis=-1, keepdims=True)
        centered = values_f - row_mean
        row_var = jnp.mean(centered * centered, axis=-1, keepdims=True)
        scaled = centered * lax.rsqrt(row_var + 1e-06)
        normed[...] = (scaled * (1.0 + mod[1:2, :]) + mod[0:1, :]).astype(jnp.bfloat16)

    projected = jnp.dot(normed[...], w_qkv[...], preferred_element_type=jnp.float32).astype(
        jnp.bfloat16
    )
    patch_here = facts[base + 1]
    keep = facts[base + 2].astype(jnp.float32)
    blank = jnp.zeros((PATCH, HD), jnp.bfloat16)
    mixed = []
    for head in range(block_heads):
        query = projected[:, head * 3 * HD : head * 3 * HD + HD]
        pair = projected[:, head * 3 * HD + HD : (head + 1) * 3 * HD]
        lanes = slice(head * 2 * HD, (head + 1) * 2 * HD)
        fresh_out[:, lanes] = (pair.astype(jnp.float32) * keep).astype(jnp.bfloat16)
        query = jnp.concatenate([query * jnp.bfloat16(HD**-0.5), blank], axis=1)
        pairs = [pair]
        for number in range(PATCHES - 1):
            place = number + (number >= patch_here).astype(jnp.int32)
            pairs.append(stale[pl.ds(pl.multiple_of(place * PATCH, PATCH), PATCH), lanes])
        pairs.append(stale[PATCHES * PATCH :, lanes])
        scores = [nt_dot(query, part) for part in pairs]
        top = functools.reduce(
            jnp.maximum, [jnp.max(part, axis=-1, keepdims=True) for part in scores]
        )
        exponent = [jnp.exp(part - top) for part in scores]
        norm = sum(jnp.sum(part, axis=-1, keepdims=True) for part in exponent)
        values = sum(
            jnp.dot(part.astype(jnp.bfloat16), kv, preferred_element_type=jnp.float32)
            for part, kv in zip(exponent, pairs)
        )
        mixed.append((values[:, HD:] / norm).astype(jnp.bfloat16))
    terms = nt_dot(jnp.concatenate(mixed, axis=1), w_out[...])

    @pl.when(step == 0)
    def _():
        total[...] = terms

    @pl.when(step > 0)
    def _():
        total[...] += terms

    @pl.when(step == pl.num_programs(0) - 1)
    def _():
        out_terms[...] = total[...].astype(jnp.bfloat16)


def run_layer(tick, facts, hidden, modulation, w_qkv, stale_kv, w_out, fresh_buf):
    width = hidden.shape[2]
    heads_here = stale_kv.shape[-1] // (2 * HD)
    block_heads = 4 if heads_here % 4 == 0 else heads_here
    items = modulation.shape[0]
    base = 3 * tick
    operands = [facts, hidden, modulation, w_qkv, stale_kv, w_out]
    in_specs = [
        pl.BlockSpec((None, PATCH, width), lambda i, f: (0, 0, 0)),
        pl.BlockSpec((None, 3, width), lambda i, f: (f[base], 0, 0)),
        pl.BlockSpec((width, block_heads * 3 * HD), lambda i, f: (0, i)),
        pl.BlockSpec(
            (None, None, None, STALE, block_heads * 2 * HD),
            lambda i, f: (0, f[base] // 2, f[base] % 2, 0, i),
        ),
        pl.BlockSpec((width, block_heads * HD), lambda i, f: (0, i)),
    ]
    aliases = {}
    if fresh_buf is not None:
        aliases = {len(operands): 0}
        operands.append(fresh_buf)
        in_specs.append(pl.BlockSpec(memory_space=pl.ANY))
    return pl.pallas_call(
        functools.partial(layer_kernel, block_heads, base),
        out_shape=(
            jax.ShapeDtypeStruct((items, PATCH, heads_here * 2 * HD), jnp.bfloat16),
            jax.ShapeDtypeStruct((PATCH, width), jnp.bfloat16),
        ),
        grid_spec=pltpu.PrefetchScalarGridSpec(
            num_scalar_prefetch=1,
            grid=(heads_here // block_heads,),
            in_specs=in_specs,
            out_specs=[
                pl.BlockSpec((None, PATCH, block_heads * 2 * HD), lambda i, f: (f[base], 0, i)),
                pl.BlockSpec((PATCH, width), lambda i, f: (0, 0)),
            ],
            scratch_shapes=[
                pltpu.VMEM((PATCH, width), jnp.bfloat16),
                pltpu.VMEM((PATCH, width), jnp.float32),
            ],
        ),
        input_output_aliases=aliases,
        compiler_params=pltpu.CompilerParams(vmem_limit_bytes=48 << 20),
    )(*operands)


def exchange_kernel(heads, sections, next_item, terms, hidden, mods, tokens, *rest):
    sends = next_item is not None
    if sends:
        kept, following, mine, inbox, h_send, h_recv, s_send, s_recv, f_send, f_recv, o_sem = rest
    else:
        kept, inbox, h_send, h_recv = rest
    me = lax.axis_index("head")
    section = lax.axis_index("section")
    rows = kept.shape[0]
    chunks = max(1, rows // 32)
    size = rows // chunks

    barrier = pltpu.get_barrier_semaphore()
    for far in range(1, heads):
        peer = {"head": (me + far) % heads}
        pl.semaphore_signal(barrier, inc=1, device_id=peer, device_id_type=MESH)
    if sends:

        @pl.when(section > 0)
        def _():
            peer = {"section": section - 1}
            pl.semaphore_signal(barrier, inc=1, device_id=peer, device_id_type=MESH)

    greeted = heads - 1
    if sends:
        greeted = greeted + (section < sections - 1).astype(jnp.int32)
    pl.semaphore_wait(barrier, greeted)

    def rows_of(device, chunk):
        return pl.ds(pl.multiple_of(device * rows + chunk * size, size), size)

    def share(far, chunk):
        peer = (me + far) % heads
        return pltpu.make_async_remote_copy(
            src_ref=terms.at[rows_of(peer, chunk)],
            dst_ref=inbox.at[far - 1, pl.ds(chunk * size, size)],
            send_sem=h_send.at[far - 1, chunk],
            recv_sem=h_recv.at[far - 1, chunk],
            device_id={"head": peer},
            device_id_type=MESH,
        )

    def onward(chunk):
        return pltpu.make_async_remote_copy(
            src_ref=mine.at[pl.ds(chunk * size, size)],
            dst_ref=following.at[rows_of(me, chunk)],
            send_sem=s_send.at[chunk],
            recv_sem=s_recv.at[chunk],
            device_id={"section": section + 1},
            device_id_type=MESH,
        )

    def arrived(chunk):
        return pltpu.make_async_remote_copy(
            src_ref=mine.at[pl.ds(chunk * size, size)],
            dst_ref=following.at[rows_of(me, chunk)],
            send_sem=s_send.at[chunk],
            recv_sem=s_recv.at[chunk],
            device_id={"section": section - 1},
            device_id_type=MESH,
        )

    def forward(far, chunk, owner):
        return pltpu.make_async_remote_copy(
            src_ref=following.at[rows_of(owner, chunk)],
            dst_ref=following.at[rows_of(owner, chunk)],
            send_sem=f_send.at[far - 1, chunk],
            recv_sem=f_recv.at[far - 1, chunk],
            device_id={"head": (me + far) % heads},
            device_id_type=MESH,
        )

    for chunk in range(chunks):
        for far in range(1, heads):
            share(far, chunk).start()
    if sends:
        own = pltpu.make_async_copy(tokens.at[next_item], following, o_sem)

        @pl.when(section == 0)
        def _():
            own.start()

    gate = mods[0:1, :]
    keep = mods[1:2, :]
    for chunk in range(chunks):
        attn = terms[rows_of(me, chunk), :].astype(jnp.float32)
        for far in range(1, heads):
            share(far, chunk).wait_recv()
            attn = attn + inbox[far - 1, chunk * size : (chunk + 1) * size, :].astype(jnp.float32)
        before = hidden[rows_of(me, chunk), :].astype(jnp.float32)
        updated = (before + gate * attn).astype(jnp.bfloat16)
        kept[chunk * size : (chunk + 1) * size, :] = (updated.astype(jnp.float32) * keep).astype(
            jnp.bfloat16
        )
        if sends:
            mine[chunk * size : (chunk + 1) * size, :] = updated

            @pl.when(section < sections - 1)
            def _():
                onward(chunk).start()

    if sends:

        @pl.when(section > 0)
        def _():
            for chunk in range(chunks):
                arrived(chunk).wait_recv()
                for far in range(1, heads):
                    forward(far, chunk, me).start()
            for chunk in range(chunks):
                for far in range(1, heads):
                    forward(far, chunk, (me + heads - far) % heads).wait_recv()
                    forward(far, chunk, me).wait_send()

        @pl.when(section < sections - 1)
        def _():
            for chunk in range(chunks):
                onward(chunk).wait_send()

        @pl.when(section == 0)
        def _():
            own.wait()

    for chunk in range(chunks):
        for far in range(1, heads):
            share(far, chunk).wait_send()


def exchange(tick, next_item, terms, hidden, mods, tokens):
    heads = lax.axis_size("head")
    sections = lax.axis_size("section")
    width = terms.shape[1]
    rows = PATCH // heads
    chunks = max(1, rows // 32)
    vmem = pl.BlockSpec(memory_space=pltpu.VMEM)
    dma = pltpu.SemaphoreType.DMA
    out_shape = [jax.ShapeDtypeStruct((rows, width), jnp.bfloat16)]
    scratch = [
        pltpu.VMEM((heads - 1, rows, width), jnp.bfloat16),
        dma((heads - 1, chunks)),
        dma((heads - 1, chunks)),
    ]
    if next_item is not None:
        out_shape.append(jax.ShapeDtypeStruct((PATCH, width), jnp.bfloat16))
        scratch = [
            pltpu.VMEM((rows, width), jnp.bfloat16),
            *scratch,
            dma((chunks,)),
            dma((chunks,)),
            dma((heads - 1, chunks)),
            dma((heads - 1, chunks)),
            dma,
        ]
    return pl.pallas_call(
        functools.partial(exchange_kernel, heads, sections, next_item),
        out_shape=out_shape,
        in_specs=[
            vmem,
            vmem,
            vmem,
            pl.BlockSpec(memory_space=pl.ANY),
        ],
        out_specs=[vmem] * len(out_shape),
        scratch_shapes=scratch,
        compiler_params=pltpu.CompilerParams(
            collective_id=1 + tick, has_side_effects=True, vmem_limit_bytes=32 << 20
        ),
    )(terms, hidden, mods, tokens)


def shards(
    latent_tokens, w_qkv, w_out, time_mod, text_mod, stale_kv, guided, patch_index, timestep
):
    section_index = lax.axis_index("section")
    sections = lax.axis_size("section")
    requests = latent_tokens.shape[0]
    item_count = 2 * requests
    local_rows, model_width = latent_tokens.shape[2:]
    tokens = latent_tokens.reshape(item_count, local_rows, model_width)
    tokens_full = lax.all_gather(tokens, "head", axis=1, tiled=True)
    per_time = jnp.stack(
        [
            lax.dynamic_index_in_dim(time_mod[0], timestep[i], 0, keepdims=False)
            for i in range(requests)
        ]
    )
    modulation = (per_time[:, None] + text_mod[0]).reshape(item_count, 3, model_width)
    patch_all = jnp.repeat(patch_index, 2)
    guided_all = jnp.repeat(guided, 2)
    parity = jnp.arange(item_count, dtype=jnp.int32) % 2
    keep_all = jnp.where((parity == 1) & (guided_all == 0), 0, 1).astype(jnp.int32)
    qkv_all, out_all = gather_weights(w_qkv[0], w_out[0].T)
    qkv_full = qkv_all.reshape(-1, qkv_all.shape[-1])
    out_full = out_all.reshape(-1, out_all.shape[-1])

    ticks = item_count + sections - 1
    slots = [jnp.clip(tick - section_index, 0, item_count - 1) for tick in range(ticks)]
    facts = jnp.stack([part for s in slots for part in (s, patch_all[s], keep_all[s])])
    mods = [
        jnp.stack(
            [
                lax.dynamic_index_in_dim(modulation[:, 2], s, 0, keepdims=False),
                jnp.full((model_width,), keep_all[s].astype(jnp.float32)),
            ]
        )
        for s in slots
    ]
    fresh_buf = None
    hidden = tokens_full
    kept = []
    for tick in range(ticks):
        fresh_buf, out_terms = run_layer(
            tick, facts, hidden, modulation, qkv_full, stale_kv, out_full, fresh_buf
        )
        next_item = min(tick + 1, item_count - 1) if tick < ticks - 1 else None
        result = exchange(tick, next_item, out_terms, hidden[0], mods[tick], tokens_full)
        kept.append(result[0])
        if next_item is not None:
            hidden = result[1][None]
    hidden_out = jnp.stack(
        [
            lax.select_n(section_index, *(kept[i + s] for s in range(sections)))
            if sections > 2
            else jnp.where(section_index == 0, kept[i], kept[i + sections - 1])
            for i in range(item_count)
        ]
    ).reshape(1, requests, 2, local_rows, model_width)
    fresh_kv = fresh_buf.reshape(1, requests, 2, PATCH, fresh_buf.shape[-1])
    return (hidden_out, fresh_kv)


def solution(mesh):
    in_specs = (
        P("req", None, "head", None),
        P("section", "req", "head"),
        P("section", "head", "req"),
        P("section", None, None, None),
        P("section", "req", None, None, None),
        P("section", "req", None, None, "head"),
        P("req"),
        P("req"),
        P("req"),
    )
    out_specs = (P("section", "req", None, "head", None), P("section", "req", None, None, "head"))
    return jax.shard_map(shards, mesh=mesh, in_specs=in_specs, out_specs=out_specs, check_vma=False)
```

```python
import functools

import jax
import jax.numpy as jnp
from jax import lax
from jax.experimental import pallas as pl
from jax.experimental.pallas import tpu as pltpu
from jax.sharding import PartitionSpec as P

HD = 64
PATCH = 256
PATCHES = 4
STALE = 1178
TEXT = STALE - PATCHES * PATCH
MESH = pl.DeviceIdType.MESH


def ring_index(place, n):
    return jnp.where(place < n // 2, 2 * place, 2 * (n - 1 - place) + 1)


def gather_kernel(n, qkv_ref, out_ref, qkv_all, out_all, send_sem, recv_sem, own_sem):
    me = lax.axis_index("req")
    place = jnp.where(me % 2 == 0, me // 2, n - 1 - me // 2)
    right = ring_index((place + 1) % n, n)
    left = ring_index((place + n - 1) % n, n)
    barrier = pltpu.get_barrier_semaphore()
    for neighbour in (left, right):
        pl.semaphore_signal(barrier, inc=1, device_id={"req": neighbour}, device_id_type=MESH)
    pl.semaphore_wait(barrier, 2)

    rows = qkv_ref.shape[0]
    out_rows = out_ref.shape[0]
    q_half, o_half = rows // 2, out_rows // 2
    q_cut = (q_half // 2 + 7) // 8 * 8
    pieces = []
    for way in range(2):
        pieces.append(
            (
                (qkv_ref, qkv_all, way * q_half, q_cut),
                (qkv_ref, qkv_all, way * q_half + q_cut, q_half - q_cut),
                (out_ref, out_all, way * o_half, o_half),
            )
        )
    own = (
        pltpu.make_async_copy(qkv_ref, qkv_all.at[me], own_sem.at[0]),
        pltpu.make_async_copy(out_ref, out_all.at[me], own_sem.at[1]),
    )

    def hop(step, way, number):
        source, target, first, count = pieces[way][number]
        owner = ring_index((place + (n - step if way == 0 else step)) % n, n)
        span = pl.ds(first, count)
        block = source.at[span] if step == 0 else target.at[owner, span]
        return pltpu.make_async_remote_copy(
            src_ref=block,
            dst_ref=target.at[owner, span],
            send_sem=send_sem.at[way, number],
            recv_sem=recv_sem.at[step, way, number],
            device_id={"req": right if way == 0 else left},
            device_id_type=MESH,
        )

    for step in range(n - 1):
        for number in range(3):
            for way in range(2):
                if step > 0:
                    before = hop(step - 1, way, number)
                    before.wait_recv()
                    before.wait_send()
                hop(step, way, number).start()
        if step == 0:
            for copy in own:
                copy.start()
    for number in range(3):
        for way in range(2):
            last = hop(n - 2, way, number)
            last.wait_recv()
            last.wait_send()
    for copy in own:
        copy.wait()


def gather_weights(qkv_shard, out_shard):
    n = lax.axis_size("req")
    return pl.pallas_call(
        functools.partial(gather_kernel, n),
        out_shape=(
            jax.ShapeDtypeStruct((n, *qkv_shard.shape), qkv_shard.dtype),
            jax.ShapeDtypeStruct((n, *out_shard.shape), out_shard.dtype),
        ),
        in_specs=[pl.BlockSpec(memory_space=pl.ANY)] * 2,
        out_specs=[pl.BlockSpec(memory_space=pl.ANY)] * 2,
        scratch_shapes=[
            pltpu.SemaphoreType.DMA((2, 3)),
            pltpu.SemaphoreType.DMA((n - 1, 2, 3)),
            pltpu.SemaphoreType.DMA((2,)),
        ],
        compiler_params=pltpu.CompilerParams(collective_id=0, has_side_effects=True),
    )(qkv_shard, out_shard)


def nt_dot(a, b):
    return lax.dot_general(a, b, (((1,), (1,)), ((), ())), preferred_element_type=jnp.float32)


def layer_kernel(
    block_heads, base, facts, hidden, mod, w_qkv, stale, w_out, *rest
):
    fresh_out, out_terms, normed, total = rest[-4:]
    step = pl.program_id(0)

    @pl.when(step == 0)
    def _():
        values_f = hidden[...].astype(jnp.float32)
        row_mean = jnp.mean(values_f, axis=-1, keepdims=True)
        centered = values_f - row_mean
        row_var = jnp.mean(centered * centered, axis=-1, keepdims=True)
        scaled = centered * lax.rsqrt(row_var + 1e-06)
        normed[...] = (scaled * (1.0 + mod[1:2, :]) + mod[0:1, :]).astype(jnp.bfloat16)

    projected = jnp.dot(normed[...], w_qkv[...], preferred_element_type=jnp.float32).astype(
        jnp.bfloat16
    )
    patch_here = facts[base + 1]
    keep = facts[base + 2].astype(jnp.float32)
    blank = jnp.zeros((PATCH, HD), jnp.bfloat16)
    mixed = []
    for head in range(block_heads):
        query = projected[:, head * 3 * HD : head * 3 * HD + HD]
        pair = projected[:, head * 3 * HD + HD : (head + 1) * 3 * HD]
        lanes = slice(head * 2 * HD, (head + 1) * 2 * HD)
        fresh_out[:, lanes] = (pair.astype(jnp.float32) * keep).astype(jnp.bfloat16)
        query = jnp.concatenate([query * jnp.bfloat16(HD**-0.5), blank], axis=1)
        pairs = [pair]
        for number in range(PATCHES - 1):
            place = number + (number >= patch_here).astype(jnp.int32)
            pairs.append(stale[pl.ds(pl.multiple_of(place * PATCH, PATCH), PATCH), lanes])
        pairs.append(stale[PATCHES * PATCH :, lanes])
        scores = [nt_dot(query, part) for part in pairs]
        top = functools.reduce(
            jnp.maximum, [jnp.max(part, axis=-1, keepdims=True) for part in scores]
        )
        exponent = [jnp.exp(part - top) for part in scores]
        norm = sum(jnp.sum(part, axis=-1, keepdims=True) for part in exponent)
        values = sum(
            jnp.dot(part.astype(jnp.bfloat16), kv, preferred_element_type=jnp.float32)
            for part, kv in zip(exponent, pairs)
        )
        mixed.append((values[:, HD:] / norm).astype(jnp.bfloat16))
    terms = nt_dot(jnp.concatenate(mixed, axis=1), w_out[...])

    @pl.when(step == 0)
    def _():
        total[...] = terms

    @pl.when(step > 0)
    def _():
        total[...] += terms

    @pl.when(step == pl.num_programs(0) - 1)
    def _():
        out_terms[...] = total[...].astype(jnp.bfloat16)


def run_layer(tick, facts, hidden, modulation, w_qkv, stale_kv, w_out, fresh_buf):
    width = hidden.shape[2]
    heads_here = stale_kv.shape[-1] // (2 * HD)
    block_heads = 6 if heads_here % 6 == 0 else heads_here
    items = modulation.shape[0]
    base = 3 * tick
    operands = [facts, hidden, modulation, w_qkv, stale_kv, w_out]
    in_specs = [
        pl.BlockSpec((None, PATCH, width), lambda i, f: (0, 0, 0)),
        pl.BlockSpec((None, 3, width), lambda i, f: (f[base], 0, 0)),
        pl.BlockSpec((width, block_heads * 3 * HD), lambda i, f: (0, i)),
        pl.BlockSpec(
            (None, None, None, STALE, block_heads * 2 * HD),
            lambda i, f: (0, f[base] // 2, f[base] % 2, 0, i),
        ),
        pl.BlockSpec((width, block_heads * HD), lambda i, f: (0, i)),
    ]
    aliases = {}
    if fresh_buf is not None:
        aliases = {len(operands): 0}
        operands.append(fresh_buf)
        in_specs.append(pl.BlockSpec(memory_space=pl.ANY))
    return pl.pallas_call(
        functools.partial(layer_kernel, block_heads, base),
        out_shape=(
            jax.ShapeDtypeStruct((items, PATCH, heads_here * 2 * HD), jnp.bfloat16),
            jax.ShapeDtypeStruct((PATCH, width), jnp.bfloat16),
        ),
        grid_spec=pltpu.PrefetchScalarGridSpec(
            num_scalar_prefetch=1,
            grid=(heads_here // block_heads,),
            in_specs=in_specs,
            out_specs=[
                pl.BlockSpec((None, PATCH, block_heads * 2 * HD), lambda i, f: (f[base], 0, i)),
                pl.BlockSpec((PATCH, width), lambda i, f: (0, 0)),
            ],
            scratch_shapes=[
                pltpu.VMEM((PATCH, width), jnp.bfloat16),
                pltpu.VMEM((PATCH, width), jnp.float32),
            ],
        ),
        input_output_aliases=aliases,
        compiler_params=pltpu.CompilerParams(vmem_limit_bytes=48 << 20),
    )(*operands)


def exchange_kernel(heads, sections, next_item, terms, hidden, mods, tokens, *rest):
    sends = next_item is not None
    if sends:
        kept, following, mine, inbox, h_send, h_recv, s_send, s_recv, f_send, f_recv, o_sem = rest
    else:
        kept, inbox, h_send, h_recv = rest
    me = lax.axis_index("head")
    section = lax.axis_index("section")
    rows = kept.shape[0]
    chunks = max(1, rows // 32)
    size = rows // chunks

    barrier = pltpu.get_barrier_semaphore()
    for far in range(1, heads):
        peer = {"head": (me + far) % heads}
        pl.semaphore_signal(barrier, inc=1, device_id=peer, device_id_type=MESH)
    if sends:

        @pl.when(section > 0)
        def _():
            peer = {"section": section - 1}
            pl.semaphore_signal(barrier, inc=1, device_id=peer, device_id_type=MESH)

    greeted = heads - 1
    if sends:
        greeted = greeted + (section < sections - 1).astype(jnp.int32)
    pl.semaphore_wait(barrier, greeted)

    def rows_of(device, chunk):
        return pl.ds(pl.multiple_of(device * rows + chunk * size, size), size)

    def share(far, chunk):
        peer = (me + far) % heads
        return pltpu.make_async_remote_copy(
            src_ref=terms.at[rows_of(peer, chunk)],
            dst_ref=inbox.at[far - 1, pl.ds(chunk * size, size)],
            send_sem=h_send.at[far - 1, chunk],
            recv_sem=h_recv.at[far - 1, chunk],
            device_id={"head": peer},
            device_id_type=MESH,
        )

    def onward(chunk):
        return pltpu.make_async_remote_copy(
            src_ref=mine.at[pl.ds(chunk * size, size)],
            dst_ref=following.at[rows_of(me, chunk)],
            send_sem=s_send.at[chunk],
            recv_sem=s_recv.at[chunk],
            device_id={"section": section + 1},
            device_id_type=MESH,
        )

    def arrived(chunk):
        return pltpu.make_async_remote_copy(
            src_ref=mine.at[pl.ds(chunk * size, size)],
            dst_ref=following.at[rows_of(me, chunk)],
            send_sem=s_send.at[chunk],
            recv_sem=s_recv.at[chunk],
            device_id={"section": section - 1},
            device_id_type=MESH,
        )

    def forward(far, chunk, owner):
        return pltpu.make_async_remote_copy(
            src_ref=following.at[rows_of(owner, chunk)],
            dst_ref=following.at[rows_of(owner, chunk)],
            send_sem=f_send.at[far - 1, chunk],
            recv_sem=f_recv.at[far - 1, chunk],
            device_id={"head": (me + far) % heads},
            device_id_type=MESH,
        )

    for chunk in range(chunks):
        for far in range(1, heads):
            share(far, chunk).start()
    if sends:
        own = pltpu.make_async_copy(tokens.at[next_item], following, o_sem)

        @pl.when(section == 0)
        def _():
            own.start()

    gate = mods[0:1, :]
    keep = mods[1:2, :]
    for chunk in range(chunks):
        attn = terms[rows_of(me, chunk), :].astype(jnp.float32)
        for far in range(1, heads):
            share(far, chunk).wait_recv()
            attn = attn + inbox[far - 1, chunk * size : (chunk + 1) * size, :].astype(jnp.float32)
        before = hidden[rows_of(me, chunk), :].astype(jnp.float32)
        updated = (before + gate * attn).astype(jnp.bfloat16)
        kept[chunk * size : (chunk + 1) * size, :] = (updated.astype(jnp.float32) * keep).astype(
            jnp.bfloat16
        )
        if sends:
            mine[chunk * size : (chunk + 1) * size, :] = updated

            @pl.when(section < sections - 1)
            def _():
                onward(chunk).start()

    if sends:

        @pl.when(section > 0)
        def _():
            for chunk in range(chunks):
                arrived(chunk).wait_recv()
                for far in range(1, heads):
                    forward(far, chunk, me).start()
            for chunk in range(chunks):
                for far in range(1, heads):
                    forward(far, chunk, (me + heads - far) % heads).wait_recv()
                    forward(far, chunk, me).wait_send()

        @pl.when(section < sections - 1)
        def _():
            for chunk in range(chunks):
                onward(chunk).wait_send()

        @pl.when(section == 0)
        def _():
            own.wait()

    for chunk in range(chunks):
        for far in range(1, heads):
            share(far, chunk).wait_send()


def exchange(tick, next_item, terms, hidden, mods, tokens):
    heads = lax.axis_size("head")
    sections = lax.axis_size("section")
    width = terms.shape[1]
    rows = PATCH // heads
    chunks = max(1, rows // 32)
    vmem = pl.BlockSpec(memory_space=pltpu.VMEM)
    dma = pltpu.SemaphoreType.DMA
    out_shape = [jax.ShapeDtypeStruct((rows, width), jnp.bfloat16)]
    scratch = [
        pltpu.VMEM((heads - 1, rows, width), jnp.bfloat16),
        dma((heads - 1, chunks)),
        dma((heads - 1, chunks)),
    ]
    if next_item is not None:
        out_shape.append(jax.ShapeDtypeStruct((PATCH, width), jnp.bfloat16))
        scratch = [
            pltpu.VMEM((rows, width), jnp.bfloat16),
            *scratch,
            dma((chunks,)),
            dma((chunks,)),
            dma((heads - 1, chunks)),
            dma((heads - 1, chunks)),
            dma,
        ]
    return pl.pallas_call(
        functools.partial(exchange_kernel, heads, sections, next_item),
        out_shape=out_shape,
        in_specs=[
            vmem,
            vmem,
            vmem,
            pl.BlockSpec(memory_space=pl.ANY),
        ],
        out_specs=[vmem] * len(out_shape),
        scratch_shapes=scratch,
        compiler_params=pltpu.CompilerParams(
            collective_id=1 + tick, has_side_effects=True, vmem_limit_bytes=32 << 20
        ),
    )(terms, hidden, mods, tokens)


def shards(
    latent_tokens, w_qkv, w_out, time_mod, text_mod, stale_kv, guided, patch_index, timestep
):
    section_index = lax.axis_index("section")
    sections = lax.axis_size("section")
    requests = latent_tokens.shape[0]
    item_count = 2 * requests
    local_rows, model_width = latent_tokens.shape[2:]
    tokens = latent_tokens.reshape(item_count, local_rows, model_width)
    tokens_full = lax.all_gather(tokens, "head", axis=1, tiled=True)
    per_time = jnp.stack(
        [
            lax.dynamic_index_in_dim(time_mod[0], timestep[i], 0, keepdims=False)
            for i in range(requests)
        ]
    )
    modulation = (per_time[:, None] + text_mod[0]).reshape(item_count, 3, model_width)
    patch_all = jnp.repeat(patch_index, 2)
    guided_all = jnp.repeat(guided, 2)
    parity = jnp.arange(item_count, dtype=jnp.int32) % 2
    keep_all = jnp.where((parity == 1) & (guided_all == 0), 0, 1).astype(jnp.int32)
    qkv_all, out_all = gather_weights(w_qkv[0], w_out[0].T)
    qkv_full = qkv_all.reshape(-1, qkv_all.shape[-1])
    out_full = out_all.reshape(-1, out_all.shape[-1])

    ticks = item_count + sections - 1
    slots = [jnp.clip(tick - section_index, 0, item_count - 1) for tick in range(ticks)]
    slot_all = jnp.clip(jnp.arange(ticks, dtype=jnp.int32) - section_index, 0, item_count - 1)
    chosen = slot_all[:, None] == jnp.arange(item_count, dtype=jnp.int32)[None, :]
    facts = jnp.stack(
        [
            slot_all,
            jnp.sum(jnp.where(chosen, patch_all[None, :], 0), axis=1),
            jnp.sum(jnp.where(chosen, keep_all[None, :], 0), axis=1),
        ],
        axis=1,
    ).reshape(-1)
    mods = [
        jnp.stack(
            [
                lax.dynamic_index_in_dim(modulation[:, 2], s, 0, keepdims=False),
                jnp.full((model_width,), keep_all[s].astype(jnp.float32)),
            ]
        )
        for s in slots
    ]
    fresh_buf = None
    hidden = tokens_full
    kept = []
    for tick in range(ticks):
        fresh_buf, out_terms = run_layer(
            tick, facts, hidden, modulation, qkv_full, stale_kv, out_full, fresh_buf
        )
        next_item = min(tick + 1, item_count - 1) if tick < ticks - 1 else None
        result = exchange(tick, next_item, out_terms, hidden[0], mods[tick], tokens_full)
        kept.append(result[0])
        if next_item is not None:
            hidden = result[1][None]
    hidden_out = jnp.stack(
        [
            lax.select_n(section_index, *(kept[i + s] for s in range(sections)))
            if sections > 2
            else jnp.where(section_index == 0, kept[i], kept[i + sections - 1])
            for i in range(item_count)
        ]
    ).reshape(1, requests, 2, local_rows, model_width)
    fresh_kv = fresh_buf.reshape(1, requests, 2, PATCH, fresh_buf.shape[-1])
    return (hidden_out, fresh_kv)


def solution(mesh):
    in_specs = (
        P("req", None, "head", None),
        P("section", "req", "head"),
        P("section", "head", "req"),
        P("section", None, None, None),
        P("section", "req", None, None, None),
        P("section", "req", None, None, "head"),
        P("req"),
        P("req"),
        P("req"),
    )
    out_specs = (P("section", "req", None, "head", None), P("section", "req", None, None, "head"))
    return jax.shard_map(shards, mesh=mesh, in_specs=in_specs, out_specs=out_specs, check_vma=False)
```
